32 devices in a mesh: sub: 8 (over y, x, core), grp: 4 (over z).
Axes of the slice: x: 2, y: 2, z: 4, core: 2. Of those that a mesh axis runs over, the one named last changes fastest.
Arguments:
- node_rows: bfloat16 [32768, 512], P(('sub', 'grp')), may hold values from -6 to 6
- owners: int32 [32768], P(('sub', 'grp')), may hold values from 0 to 31, as said below
- tile_src: int32 [8, 4, 16, 2], P('sub', 'grp'), may hold values from 0 to 15
- neighbors: int32 [8, 4, 2048, 16], P('sub', 'grp'), may hold values from 0 to 127
- pool_pair: int32 [8, 4, 2048], P('sub', 'grp'), may hold values from 0 to 2047, each once within a row
- pool_quad: int32 [4, 4, 2048], P(None, 'grp'), may hold values from 0 to 2047, each once within a row
- pool_top: int32 [2, 4, 2048], P(None, 'grp'), may hold values from 0 to 2047, each once within a row
- edge_in: bfloat16 [2, 512, 512], replicated, may hold values from -0.25 to 0.25
- edge_bias: float32 [512], replicated, may hold values from -4 to 4
- edge_out: bfloat16 [512, 512], replicated, may hold values from -0.25 to 0.25
- node_in: bfloat16 [2, 512, 512], replicated, may hold values from -0.25 to 0.25
- node_bias: float32 [512], replicated, may hold values from -4 to 4
- node_out: bfloat16 [512, 512], replicated, may hold values from -0.25 to 0.25
- out_gain: float32 [512], replicated, may hold values from 0.1 to 1.9
- coarse: bfloat16 [3, 512, 512], replicated, may hold values from -0.25 to 0.25
Outputs:
- updated: bfloat16 [65536, 512], P(('sub', 'grp'))
The draws below stay inside these ranges and needn't reach their ends.
Inputs may be any that keep to these rules, and one draw needn't show every extreme that they name: `owners`: at most 64 nodes of one shard go to one owner, and one owner receives exactly 64 nodes from every shard. `pool_pair`: every row of the pooling map is a permutation of the 2048 slots. `pool_quad`: every row of the pooling map is a permutation of the 2048 slots. `pool_top`: every row of the pooling map is a permutation of the 2048 slots.
All inputs are finite; a program needn't handle non-finite values.
Results may differ from the reference program's by a relative error of at most 0.007.
Values may be sent and summed in bfloat16 or wider, within the bound.
A program may use at most 64 MiB of HBM per device.

```python
import jax
import jax.numpy as jnp
from jax import lax

W = 512
OWN_DEV = 2048
BLK = 128
TPB = 2
NBR = 8
OWNERS = 32
CAP = 64
NODE_DEV = 1024
NODES = 32768
BLOCKS = 16
N_SUB = 8
N_GRP = 4


def draw_owners(key, part):
    favored = jax.random.randint(jax.random.fold_in(key, 7), (), 0, OWNERS).astype(jnp.int32)
    slot_total = OWNERS * CAP

    def one_source(source):
        source_key = jax.random.fold_in(key, source + 11)
        shuffled = jax.random.permutation(jax.random.fold_in(source_key, 1), slot_total).astype(jnp.int32)
        owner_of = shuffled // CAP
        ranking = jnp.arange(slot_total, dtype=jnp.int32) + slot_total * (owner_of == favored).astype(jnp.int32)
        picked = owner_of[jnp.argsort(ranking, stable=True)[:NODE_DEV - CAP]]
        listing = jnp.concatenate([jnp.full((CAP,), favored, jnp.int32), picked.astype(jnp.int32)])
        return jax.random.permutation(jax.random.fold_in(source_key, 2), listing)
    return jax.vmap(one_source)(jnp.arange(OWNERS, dtype=jnp.int32)).reshape(-1).astype(jnp.int32)


def touch_ends(drawn, key, smallest, high):
    place = [jax.random.randint(jax.random.fold_in(key, axis), (), 0, length) for axis, length in enumerate(drawn.shape)]
    longest = drawn.shape.index(max(drawn.shape))
    next_to = place[:longest] + [(place[longest] + 1) % drawn.shape[longest]] + place[longest + 1:]
    return drawn.at[tuple(place)].set(smallest).at[tuple(next_to)].set(high)


def steps_of(stream_key, shape, split, smallest, top_value):
    loudness, own = 1.0, jax.random.fold_in(stream_key, 6)
    for dim, blocks in split:
        heights = jnp.exp(jax.random.uniform(jax.random.fold_in(own, dim), (blocks,), jnp.float32, smallest / len(split), top_value / len(split)))
        loudness = loudness * jnp.repeat(heights, shape[dim] // blocks).reshape([-1 if axis == dim else 1 for axis in range(len(shape))])
    return loudness


def normal_values(own_key, shape, width, bound, shards=(), kind=jnp.bfloat16):
    level = steps_of(own_key, shape, shards, -0.22, 0.18) if shards else 1.0
    array = jax.random.normal(own_key, shape, jnp.float32) * width * level
    return jnp.minimum(jnp.maximum(array, -bound), bound).astype(kind)


def setup_inputs(seed: int = 0) -> dict:
    streams_of = jax.random.split(jax.random.key(seed), 16)
    node_rows = normal_values(streams_of[0], (NODES, W), 1.0, 6.0, ((0, 32),))
    owners = draw_owners(jax.random.fold_in(streams_of[15], 71), 0)
    tile_src = touch_ends(jax.random.randint(streams_of[2], (N_SUB, N_GRP, BLOCKS, TPB), 0, BLOCKS), jax.random.fold_in(streams_of[2], 1), 0, BLOCKS - 1).astype(jnp.int32)
    neighbors = touch_ends(jax.random.randint(streams_of[3], (N_SUB, N_GRP, OWN_DEV, TPB * NBR), 0, BLK), jax.random.fold_in(streams_of[3], 1), 0, BLK - 1).astype(jnp.int32)
    pool_pair = jax.vmap(lambda own: jax.random.permutation(own, OWN_DEV))(jax.random.split(streams_of[4], N_SUB * N_GRP)).reshape((N_SUB, N_GRP, OWN_DEV)).astype(jnp.int32)
    pool_quad = jax.vmap(lambda own: jax.random.permutation(own, OWN_DEV))(jax.random.split(streams_of[5], (N_SUB // 2) * N_GRP)).reshape((N_SUB // 2, N_GRP, OWN_DEV)).astype(jnp.int32)
    pool_top = jax.vmap(lambda own: jax.random.permutation(own, OWN_DEV))(jax.random.split(streams_of[6], (N_SUB // 4) * N_GRP)).reshape((N_SUB // 4, N_GRP, OWN_DEV)).astype(jnp.int32)
    edge_in = normal_values(streams_of[7], (2, W, W), W ** -0.5, 0.25)
    edge_bias = normal_values(streams_of[8], (W,), 1.0, 4.0, (), jnp.float32)
    edge_out = normal_values(streams_of[9], (W, W), W ** -0.5, 0.25)
    node_in = normal_values(streams_of[10], (2, W, W), W ** -0.5, 0.25)
    node_bias = normal_values(streams_of[11], (W,), 1.0, 4.0, (), jnp.float32)
    node_out = normal_values(streams_of[12], (W, W), W ** -0.5, 0.25)
    out_gain = jnp.clip(1.0 + 0.18 * jax.random.normal(streams_of[13], (W,), jnp.float32), 0.1, 1.9)
    coarse = normal_values(streams_of[14], (3, W, W), W ** -0.5, 0.25)
    return dict(node_rows=node_rows, owners=owners, tile_src=tile_src, neighbors=neighbors, pool_pair=pool_pair, pool_quad=pool_quad, pool_top=pool_top, edge_in=edge_in, edge_bias=edge_bias, edge_out=edge_out, node_in=node_in, node_bias=node_bias, node_out=node_out, out_gain=out_gain, coarse=coarse)


epsilon = 1e-05

def place_slots(node_rows, owners):
    source_owner = owners.reshape(OWNERS, NODE_DEV)
    matches = (source_owner[:, :, None] == jnp.arange(OWNERS, dtype=jnp.int32)[None, None, :]).astype(jnp.int32)
    position = lax.optimization_barrier(jnp.sum((jnp.cumsum(matches, axis=1) - matches) * matches, axis=2))
    source_index = jnp.arange(OWNERS, dtype=jnp.int32)[:, None]
    target = (source_owner * OWN_DEV + source_index * CAP + position).reshape(-1).astype(jnp.int32)
    slots = jnp.zeros((OWNERS * OWN_DEV, W), jnp.bfloat16).at[target].set(node_rows)
    present = jnp.zeros((OWNERS * OWN_DEV,), jnp.float32).at[target].set(1.0)
    return (slots.reshape(OWNERS, OWN_DEV, W), present.reshape(OWNERS, OWN_DEV))

def block_sum(proj_dst, proj_src, present, tile_rows, near_rows, block_index):
    start = block_index * BLK
    dst_rows = lax.dynamic_slice_in_dim(proj_dst, start, BLK, 0).astype(jnp.float32)
    near_block = lax.dynamic_slice_in_dim(near_rows, start, BLK, 0)
    base = jnp.repeat(tile_rows[block_index], NBR) * BLK
    source = (base[None, :] + near_block).astype(jnp.int32)
    gathered = proj_src[source].astype(jnp.float32)
    weight = present[source]
    return lax.optimization_barrier(jnp.sum(jax.nn.silu(dst_rows[:, None, :] + gathered) * weight[:, :, None], axis=1))

def fine_update(slots, present, tile_rows, near_rows, edge_in, edge_bias, edge_out, node_in, node_bias, node_out, out_gain):
    proj_dst = (jnp.dot(slots, edge_in[0], preferred_element_type=jnp.float32) + edge_bias).astype(jnp.bfloat16)
    proj_src = jnp.dot(slots, edge_in[1], preferred_element_type=jnp.float32).astype(jnp.bfloat16)
    summed = lax.map(lambda block_index: block_sum(proj_dst, proj_src, present, tile_rows, near_rows, block_index), jnp.arange(BLOCKS, dtype=jnp.int32))
    agg = summed.reshape(OWN_DEV, W).astype(jnp.bfloat16)
    message = jnp.dot(agg, edge_out, preferred_element_type=jnp.float32).astype(jnp.bfloat16)
    hidden = jax.nn.silu(jnp.dot(slots, node_in[0], preferred_element_type=jnp.float32) + jnp.dot(message, node_in[1], preferred_element_type=jnp.float32) + node_bias).astype(jnp.bfloat16)
    delta = jnp.dot(hidden, node_out, preferred_element_type=jnp.float32)
    normed = delta * lax.rsqrt(lax.optimization_barrier(jnp.mean(delta * delta, axis=-1, keepdims=True)) + epsilon)
    return (present[:, None] * (slots.astype(jnp.float32) + out_gain * normed)).astype(jnp.bfloat16)

def refine(total, count, weight):
    mean_rows = total / jnp.maximum(count, 1.0)[..., None]
    rounded = mean_rows.astype(jnp.bfloat16)
    lifted = jnp.dot(rounded.reshape(-1, W), weight, preferred_element_type=jnp.float32).reshape(mean_rows.shape)
    return (mean_rows + jax.nn.silu(lifted)).astype(jnp.bfloat16)

def invert(perm):
    flat = perm.reshape(-1, OWN_DEV)
    inverse = jax.vmap(lambda single: jnp.zeros((OWN_DEV,), jnp.int32).at[single].set(jnp.arange(OWN_DEV, dtype=jnp.int32)))(flat)
    return inverse.reshape(perm.shape)

def pick_rows(values, perm):
    return jnp.take_along_axis(values, perm[..., None], axis=-2)

def reference(node_rows, owners, tile_src, neighbors, pool_pair, pool_quad, pool_top, edge_in, edge_bias, edge_out, node_in, node_bias, node_out, out_gain, coarse):
    slots, present = place_slots(node_rows, owners)
    tiles = tile_src.reshape(OWNERS, BLOCKS, TPB)
    nears = neighbors.reshape(OWNERS, OWN_DEV, TPB * NBR)
    fine = lax.map(lambda packed: fine_update(packed[0], packed[1], packed[2], packed[3], edge_in, edge_bias, edge_out, node_in, node_bias, node_out, out_gain), (slots, present, tiles, nears))
    fine4 = fine.reshape(N_SUB, N_GRP, OWN_DEV, W)
    present4 = present.reshape(N_SUB, N_GRP, OWN_DEV)
    count_side = jnp.take_along_axis(present4, pool_pair, axis=2)
    term = (count_side[..., None] * pick_rows(fine4, pool_pair).astype(jnp.float32)).reshape(N_SUB // 2, 2, N_GRP, OWN_DEV, W)
    counts = count_side.reshape(N_SUB // 2, 2, N_GRP, OWN_DEV)
    count1 = counts[:, 0] + counts[:, 1]
    level1 = refine(term[:, 0] + term[:, 1], count1, coarse[0])
    count_side = jnp.take_along_axis(count1, pool_quad, axis=2)
    term = (count_side[..., None] * pick_rows(level1, pool_quad).astype(jnp.float32)).reshape(N_SUB // 4, 2, N_GRP, OWN_DEV, W)
    counts = count_side.reshape(N_SUB // 4, 2, N_GRP, OWN_DEV)
    count2 = counts[:, 0] + counts[:, 1]
    level2 = refine(term[:, 0] + term[:, 1], count2, coarse[1])
    count_side = jnp.take_along_axis(count2, pool_top, axis=2)
    term = count_side[..., None] * pick_rows(level2, pool_top).astype(jnp.float32)
    level3 = refine(lax.optimization_barrier(jnp.sum(term, axis=1)), lax.optimization_barrier(jnp.sum(count_side, axis=1)), coarse[2])
    spread3 = jnp.broadcast_to(level3[:, None], (N_SUB // 4, N_GRP, OWN_DEV, W))
    back2 = (level2.astype(jnp.float32) + pick_rows(spread3, invert(pool_top)).astype(jnp.float32)).astype(jnp.bfloat16)
    back1 = (level1.astype(jnp.float32) + pick_rows(jnp.repeat(back2, 2, axis=0), invert(pool_quad)).astype(jnp.float32)).astype(jnp.bfloat16)
    lifted = pick_rows(jnp.repeat(back1, 2, axis=0), invert(pool_pair)).astype(jnp.float32)
    updated = present4[..., None] * (fine4.astype(jnp.float32) + lifted)
    return updated.reshape(OWNERS * OWN_DEV, W).astype(jnp.bfloat16)
```

```python
import functools

import jax
import jax.numpy as jnp
from jax import lax
from jax.experimental import pallas as pl
from jax.experimental.pallas import tpu as pltpu
from jax.sharding import PartitionSpec as P

BLK = 128
TPB = 2
NBR = 8
LANES = 128
PAD = 16
EMPTY = 16384.0
LIMIT = 8192.0
AWAY = -8192.0
epsilon = 1e-05
f32 = jnp.float32
bf16 = jnp.bfloat16

VM = pl.BlockSpec(memory_space=pltpu.VMEM)
SM = pl.BlockSpec(memory_space=pltpu.SMEM)


def call(kernel, outs, args, specs=None, scratch=(), flops=0):
    return pl.pallas_call(
        kernel,
        out_shape=outs,
        in_specs=specs or [VM] * len(args),
        out_specs=jax.tree.map(lambda _: VM, outs),
        scratch_shapes=list(scratch),
        compiler_params=pltpu.CompilerParams(vmem_limit_bytes=44 << 20),
        cost_estimate=pl.CostEstimate(flops=flops, bytes_accessed=8 << 20, transcendentals=0),
    )(*args)


def rows_of(shape, start=0):
    return lax.broadcasted_iota(jnp.int32, shape, 0) + start


def lanes_of(shape, start=0):
    return lax.broadcasted_iota(jnp.int32, shape, 1) + start


def one_hot(mask):
    return jnp.where(mask, 1.0, 0.0).astype(bf16)


def spread(row):
    return jnp.broadcast_to(row, (LANES, LANES)).T


def dot(a, b):
    return jnp.dot(a, b, preferred_element_type=f32)


def half_silu(h):
    return h + h * jnp.tanh(h)


def picker(perm_ref, first, count, start, width):
    tiles = []
    for c in range(0, count, LANES):
        column = spread(perm_ref[:, pl.ds(pl.multiple_of(first + c, LANES), LANES)])
        wide = jnp.concatenate([column] * (width // LANES), axis=1)
        tiles.append(one_hot(wide == lanes_of((LANES, width), start)))
    return jnp.concatenate(tiles, axis=0)


def place_kernel(cap, owners_ref, nodes_ref, out_ref):
    owner_row = owners_ref[...]
    nodes = owner_row.shape[1]
    position = jnp.zeros((1, nodes), f32)
    for c in range(0, nodes, LANES):
        column = spread(owners_ref[:, c : c + LANES])
        wide = jnp.concatenate([column] * (nodes // LANES), axis=1)
        shape = (LANES, nodes)
        earlier = (wide == owner_row) & (rows_of(shape, c) < lanes_of(shape))
        position += jnp.sum(jnp.where(earlier, 1.0, 0.0), axis=0, keepdims=True)
    target = owner_row * cap + position.astype(jnp.int32)
    tile = 256

    @pl.loop(0, out_ref.shape[0] // tile)
    def _(t):
        start = pl.multiple_of(t * tile, tile)
        mask = rows_of((tile, nodes), start) == target
        weight = jnp.where(mask, 1.0, 0.0)
        filled = jnp.max(weight, axis=1, keepdims=True)
        rows = dot(weight.astype(bf16), nodes_ref[...])
        out_ref[pl.ds(start, tile), :] = jnp.where(filled > 0.5, rows, EMPTY).astype(bf16)


def compose_kernel(pair_ref, quad_ref, top_ref, two_ref, three_ref, parts, sums):
    width = pair_ref.shape[1]
    tile = 256

    def compose(outer, inner_row, out_ref):
        which = rows_of((8, width))
        high = (outer >> 7).astype(f32)
        low = (outer & 127).astype(f32)
        parts[...] = jnp.where(which == 0, high, jnp.where(which == 1, low, 0.0))
        sums[...] = jnp.zeros_like(sums)

        @pl.loop(0, width // tile)
        def _(t):
            start = pl.multiple_of(t * tile, tile)
            sel = one_hot(rows_of((tile, width), start) == inner_row)
            sums[...] += dot(parts[:, pl.ds(start, tile)].astype(bf16), sel)

        total = sums[...]
        out_ref[...] = (total[0:1] * 128.0 + total[1:2]).astype(jnp.int32)

    compose(pair_ref[...], quad_ref[...], two_ref)
    compose(two_ref[...], top_ref[...], three_ref)


def fine_kernel(
    tile_ref,
    arrived_ref,
    near_ref,
    pair_ref,
    edge_in_ref,
    edge_bias_ref,
    edge_out_ref,
    node_in_ref,
    node_bias_ref,
    node_out_ref,
    gain_ref,
    fine_ref,
    side_ref,
    slots,
    dst,
    src,
    agg,
    sels,
    near_rows,
):
    count, features = fine_ref.shape
    tile = 256

    @pl.loop(0, count // tile)
    def _(t):
        here = pl.ds(pl.multiple_of(t * tile, tile), tile)
        raw = arrived_ref[here, :].astype(f32)
        present = raw[:, 0:1] < LIMIT
        rows = jnp.where(present, raw, 0.0).astype(bf16)
        slots[here, :] = rows
        to_dst = (dot(rows, edge_in_ref[0]) + edge_bias_ref[...]) * 0.5
        dst[here, :] = to_dst.astype(bf16)
        from_src = dot(rows, edge_in_ref[1]) * 0.5
        src[here, :] = jnp.where(present, from_src, AWAY).astype(bf16)

    group = 16

    @pl.loop(0, count // BLK)
    def _(b):
        start = pl.multiple_of(b * BLK, BLK)
        near = near_ref[pl.ds(start, BLK), :]
        for j in range(TPB):
            for k in range(NBR):
                at = j * NBR + k
                mask = near[:, at : at + 1] == lanes_of((BLK, BLK))
                sels[k * BLK : (k + 1) * BLK, :] = one_hot(mask)
            first = pl.multiple_of(tile_ref[b, j] * BLK, BLK)
            near_rows[j * NBR * BLK : (j + 1) * NBR * BLK, :] = dot(
                sels[...], src[pl.ds(first, BLK), :]
            )
        for r in range(0, BLK, group):
            here = dst[pl.ds(start + r, group), :].astype(f32)
            total = jnp.zeros((group, features), f32)
            for at in range(TPB * NBR):
                total += half_silu(here + near_rows[at * BLK + r : at * BLK + r + group, :])
            agg[pl.ds(start + r, group), :] = total.astype(bf16)

    @pl.loop(0, count // tile)
    def _(t):
        here = pl.ds(pl.multiple_of(t * tile, tile), tile)
        rows = slots[here, :]
        message = dot(agg[here, :], edge_out_ref[...]).astype(bf16)
        lifted = dot(rows, node_in_ref[0]) + dot(message, node_in_ref[1]) + node_bias_ref[...]
        hidden = half_silu(lifted * 0.5).astype(bf16)
        delta = dot(hidden, node_out_ref[...])
        scale = lax.rsqrt(jnp.mean(delta * delta, axis=-1, keepdims=True) + epsilon)
        fine = rows.astype(f32) + gain_ref[...] * (delta * scale)
        present = arrived_ref[here, 0:LANES].astype(f32)[:, 0:1] < LIMIT
        fine_ref[here, :] = jnp.where(present, fine, EMPTY).astype(bf16)

    many = 512

    @pl.loop(0, count // many)
    def _(t):
        start = pl.multiple_of(t * many, many)
        sel = picker(pair_ref, start, many, 0, count)
        side_ref[pl.ds(start, many), :] = dot(sel, fine_ref[...]).astype(bf16)


def refined(total, count, weight):
    mean_rows = total * (1.0 / jnp.maximum(count, 1.0))
    lifted = dot(mean_rows.astype(bf16), weight)
    return mean_rows + half_silu(lifted * 0.5)


def widened(column, features):
    return jnp.concatenate([column] * (features // LANES), axis=1)


def put_counts(out_ref, rows, columns):
    features = out_ref.shape[1]
    per = features // LANES
    lines = []
    for c in range(0, len(columns), per):
        lines.append(jnp.concatenate([col.T[0:1, :] for col in columns[c : c + per]], axis=1))
    which = rows_of((PAD, features))
    tail = jnp.zeros((PAD, features), f32)
    for i, line in enumerate(lines):
        tail = jnp.where(which == i, line, tail)
    out_ref[rows : rows + PAD, :] = tail.astype(bf16)


def get_count(tail, c):
    features = tail.shape[1]
    line, lane = c // features, c % features
    return spread(tail[line : line + 1, lane : lane + LANES])


def one_kernel(pick_ref, side_ref, other_ref, weight_ref, level_ref, out_ref, wide):
    count, features = level_ref.shape
    tile = 256

    @pl.loop(0, count // tile)
    def _(t):
        here = pl.ds(pl.multiple_of(t * tile, tile), tile)
        a = side_ref[here, :].astype(f32)
        b = other_ref[here, :].astype(f32)
        in_a = a[:, 0:1] < LIMIT
        in_b = b[:, 0:1] < LIMIT
        total = jnp.where(in_a, a, 0.0) + jnp.where(in_b, b, 0.0)
        marks = jnp.where(in_a, 1.0, 0.0) + jnp.where(in_b, 1.0, 0.0)
        level = refined(total, marks, weight_ref[...]).astype(bf16)
        level_ref[here, :] = level
        wide[here, 0:features] = level
        wide[here, features : features + LANES] = jnp.broadcast_to(marks, (tile, LANES)).astype(
            bf16
        )

    picked = pick_ref.shape[1]
    many = 512
    columns = []
    for start in range(0, picked, many):
        sel = picker(pick_ref, start, many, 0, count)
        got = dot(sel, wide[...])
        out_ref[start : start + many, :] = got[:, 0:features].astype(bf16)
        for c in range(0, many, LANES):
            columns.append(got[c : c + LANES, features : features + LANES])
    put_counts(out_ref, picked, columns)


def two_kernel(mine_ref, other_ref, weight_ref, out_ref):
    count = out_ref.shape[0] - PAD
    features = out_ref.shape[1]
    mine_tail = mine_ref[count : count + PAD, :].astype(f32)
    other_tail = other_ref[count : count + PAD, :].astype(f32)
    columns = []
    for c in range(0, count, LANES):
        a, b = get_count(mine_tail, c), get_count(other_tail, c)
        columns.append(a + b)
        total = widened(a, features) * mine_ref[c : c + LANES, :].astype(f32) + widened(
            b, features
        ) * other_ref[c : c + LANES, :].astype(f32)
        level = refined(total, widened(a + b, features), weight_ref[...])
        out_ref[c : c + LANES, :] = level.astype(bf16)
    put_counts(out_ref, count, columns)


def pick_kernel(place_ref, pick_ref, mine_ref, other_ref, out_ref, wide):
    count = mine_ref.shape[0] - PAD
    features = out_ref.shape[1]
    picked = pick_ref.shape[1]
    core = place_ref[0] % 2
    for piece, (ref, half) in enumerate(((mine_ref, core), (other_ref, 1 - core))):
        base = pl.multiple_of(half * count, LANES)
        wide[pl.ds(base, count), 0:features] = ref[0:count, :]
        tail = ref[count : count + PAD, :].astype(f32)
        for c in range(0, count, LANES):
            wide[pl.ds(base + c, LANES), features : features + LANES] = get_count(tail, c).astype(
                bf16
            )
    sel = picker(pick_ref, 0, picked, 0, 2 * count)
    got = dot(sel, wide[...])
    out_ref[0:picked, :] = got[:, 0:features].astype(bf16)
    put_counts(
        out_ref,
        picked,
        [got[c : c + LANES, features : features + LANES] for c in range(0, picked, LANES)],
    )


def three_kernel(all_ref, weight_ref, out_ref):
    groups = all_ref.shape[0]
    count, features = out_ref.shape
    tails = [all_ref[g, count : count + PAD, :].astype(f32) for g in range(groups)]
    for c in range(0, count, LANES):
        total, marks = 0.0, 0.0
        for g in range(groups):
            got = get_count(tails[g], c)
            marks = marks + got
            total = total + widened(got, features) * all_ref[g, c : c + LANES, :].astype(f32)
        level = refined(total, widened(marks, features), weight_ref[...])
        out_ref[c : c + LANES, :] = level.astype(bf16)


def back_kernel(last, order, place_ref, perm_ref, base_ref, *refs):
    pieces, out_ref = refs[:-1], refs[-1]
    width = perm_ref.shape[1]
    size = width // len(pieces)
    tile = 256

    @pl.loop(0, out_ref.shape[0] // tile)
    def _(t):
        start = pl.multiple_of(t * tile, tile)
        here = pl.ds(start, tile)
        base = base_ref[here, :].astype(f32)
        total = base
        for piece, flip in zip(pieces, order):
            at = (place_ref[0] % len(pieces)) ^ flip
            targets = perm_ref[:, pl.ds(pl.multiple_of(at * size, LANES), size)]
            sel = one_hot(rows_of((tile, size), start) == targets)
            total = total + dot(sel, piece[0:size, :])
        absent = 0.0 if last else EMPTY
        out_ref[here, :] = jnp.where(base[:, 0:1] < LIMIT, total, absent).astype(bf16)


def swapped(shard, flip):
    count = lax.axis_size("sub")
    return lax.ppermute(shard, "sub", [(i, i ^ flip) for i in range(count)])


def body(
    node_rows,
    owners,
    tile_src,
    neighbors,
    pool_pair,
    pool_quad,
    pool_top,
    edge_in,
    edge_bias,
    edge_out,
    node_in,
    node_bias,
    node_out,
    out_gain,
    coarse,
):
    owner_count = lax.axis_size("sub") * lax.axis_size("grp")
    slot_rows = neighbors.shape[2]
    nodes, features = node_rows.shape
    cap = slot_rows // owner_count
    me = lax.axis_index("sub")
    half, quarter = slot_rows // 2, slot_rows // 4

    def shape(rows, dtype=bf16, width=features):
        return jax.ShapeDtypeStruct((rows, width), dtype)

    placed = call(
        functools.partial(place_kernel, cap),
        shape(slot_rows),
        (owners.reshape(1, nodes), node_rows),
        flops=2 * slot_rows * nodes * features,
    )
    arrived = lax.all_to_all(
        placed.reshape(owner_count, cap, features),
        ("sub", "grp"),
        split_axis=0,
        concat_axis=0,
        tiled=True,
    ).reshape(slot_rows, features)

    pair = pool_pair.reshape(1, slot_rows)
    quad = lax.dynamic_index_in_dim(pool_quad, me // 2, 0, keepdims=False)
    top = lax.dynamic_index_in_dim(pool_top, me // 4, 0, keepdims=False)
    place = me.reshape(1).astype(jnp.int32)
    quad_half = lax.dynamic_slice_in_dim(quad, (me % 2) * half, half, 1)
    top_quarter = lax.dynamic_slice_in_dim(top, (me % 4) * quarter, quarter, 1)
    to_two, to_three = call(
        compose_kernel,
        (shape(1, jnp.int32, slot_rows), shape(1, jnp.int32, slot_rows)),
        (pair, quad, top),
        scratch=[pltpu.VMEM((8, slot_rows), f32), pltpu.VMEM((8, slot_rows), f32)],
        flops=20 * 10**9,
    )

    fine, side = call(
        fine_kernel,
        (shape(slot_rows), shape(slot_rows)),
        (
            tile_src[0, 0],
            arrived,
            neighbors[0, 0],
            pair,
            edge_in,
            edge_bias.reshape(1, features),
            edge_out,
            node_in,
            node_bias.reshape(1, features),
            node_out,
            out_gain.reshape(1, features),
        ),
        specs=[SM] + [VM] * 10,
        scratch=[pltpu.VMEM((slot_rows, features), bf16)] * 4
        + [
            pltpu.VMEM((NBR * BLK, BLK), bf16),
            pltpu.VMEM((TPB * NBR * BLK, features), f32),
        ],
        flops=40 * 10**9,
    )
    other = swapped(side, 1)
    wide = pltpu.VMEM((slot_rows, features + LANES), bf16)
    level_one, mine = call(
        one_kernel,
        (shape(slot_rows), shape(half + PAD)),
        (quad_half, side, other, coarse[0]),
        scratch=[wide],
        flops=4 * 10**9,
    )
    other = swapped(mine, 2)
    back = functools.partial(back_kernel, False)
    wide_flops = 2 * slot_rows * slot_rows * features
    raised = call(
        functools.partial(back, (0,)),
        shape(slot_rows),
        (place, pair, fine, level_one),
        specs=[SM] + [VM] * 3,
        flops=wide_flops,
    )
    mine = call(two_kernel, shape(half + PAD), (mine, other, coarse[1]), flops=10**9)
    other = swapped(mine, 1)
    chosen = call(
        pick_kernel,
        shape(quarter + PAD),
        (place, top_quarter, mine, other),
        specs=[SM] + [VM] * 3,
        scratch=[wide],
        flops=10**9,
    )
    gathered = lax.all_gather(chosen, "grp", axis=0, tiled=False)
    raised = call(
        functools.partial(back, (0, 1)),
        shape(slot_rows),
        (place, to_two, raised, mine, other),
        specs=[SM] + [VM] * 4,
        flops=wide_flops,
    )
    mine = call(three_kernel, shape(quarter), (gathered, coarse[2]), flops=10**9)
    across = swapped(mine, 2)
    return call(
        functools.partial(back_kernel, True, (0, 2, 1, 3)),
        shape(slot_rows),
        (place, to_three, raised, mine, across, swapped(mine, 1), swapped(across, 1)),
        specs=[SM] + [VM] * 6,
        flops=wide_flops,
    )


def solution(mesh):
    in_specs = (
        P(("sub", "grp"), None),
        P(("sub", "grp")),
        P("sub", "grp", None, None),
        P("sub", "grp", None, None),
        P("sub", "grp", None),
        P(None, "grp", None),
        P(None, "grp", None),
        P(),
        P(),
        P(),
        P(),
        P(),
        P(),
        P(),
        P(),
    )
    out_specs = P(("sub", "grp"), None)
    return jax.shard_map(body, mesh=mesh, in_specs=in_specs, out_specs=out_specs, check_vma=False)
```

```python
import functools

import jax
import jax.numpy as jnp
from jax import lax
from jax.experimental import pallas as pl
from jax.experimental.pallas import tpu as pltpu
from jax.sharding import PartitionSpec as P

BLK = 128
TPB = 2
NBR = 8
LANES = 128
PAD = 16
EMPTY = 16384.0
LIMIT = 8192.0
AWAY = -8192.0
epsilon = 1e-05
f32 = jnp.float32
bf16 = jnp.bfloat16

VM = pl.BlockSpec(memory_space=pltpu.VMEM)
SM = pl.BlockSpec(memory_space=pltpu.SMEM)


def call(kernel, outs, args, specs=None, scratch=(), flops=0):
    return pl.pallas_call(
        kernel,
        out_shape=outs,
        in_specs=specs or [VM] * len(args),
        out_specs=jax.tree.map(lambda _: VM, outs),
        scratch_shapes=list(scratch),
        compiler_params=pltpu.CompilerParams(vmem_limit_bytes=44 << 20),
        cost_estimate=pl.CostEstimate(flops=flops, bytes_accessed=8 << 20, transcendentals=0),
    )(*args)


def rows_of(shape, start=0):
    return lax.broadcasted_iota(jnp.int32, shape, 0) + start


def lanes_of(shape, start=0):
    return lax.broadcasted_iota(jnp.int32, shape, 1) + start


def one_hot(mask):
    return jnp.where(mask, 1.0, 0.0).astype(bf16)


def spread(row):
    return jnp.broadcast_to(row, (LANES, LANES)).T


def dot(a, b):
    return jnp.dot(a, b, preferred_element_type=f32)


def half_silu(h):
    return h + h * jnp.tanh(h)


def picker(perm_ref, first, count, start, width):
    tiles = []
    for c in range(0, count, LANES):
        column = spread(perm_ref[:, pl.ds(pl.multiple_of(first + c, LANES), LANES)])
        wide = jnp.concatenate([column] * (width // LANES), axis=1)
        tiles.append(one_hot(wide == lanes_of((LANES, width), start)))
    return jnp.concatenate(tiles, axis=0)


def place_kernel(cap, owners_ref, nodes_ref, out_ref):
    owner_row = owners_ref[...]
    nodes = owner_row.shape[1]
    position = jnp.zeros((1, nodes), f32)
    for c in range(0, nodes, LANES):
        column = spread(owners_ref[:, c : c + LANES])
        wide = jnp.concatenate([column] * (nodes // LANES), axis=1)
        shape = (LANES, nodes)
        earlier = (wide == owner_row) & (rows_of(shape, c) < lanes_of(shape))
        position += jnp.sum(jnp.where(earlier, 1.0, 0.0), axis=0, keepdims=True)
    target = owner_row * cap + position.astype(jnp.int32)
    tile = 256

    @pl.loop(0, out_ref.shape[0] // tile)
    def _(t):
        start = pl.multiple_of(t * tile, tile)
        mask = rows_of((tile, nodes), start) == target
        weight = jnp.where(mask, 1.0, 0.0)
        filled = jnp.max(weight, axis=1, keepdims=True)
        rows = dot(weight.astype(bf16), nodes_ref[...])
        out_ref[pl.ds(start, tile), :] = jnp.where(filled > 0.5, rows, EMPTY).astype(bf16)


def compose_kernel(pair_ref, quad_ref, top_ref, two_ref, three_ref, parts, sums):
    width = pair_ref.shape[1]
    tile = 256

    def compose(outer, inner_row, out_ref):
        which = rows_of((8, width))
        high = (outer >> 7).astype(f32)
        low = (outer & 127).astype(f32)
        parts[...] = jnp.where(which == 0, high, jnp.where(which == 1, low, 0.0))
        sums[...] = jnp.zeros_like(sums)

        @pl.loop(0, width // tile)
        def _(t):
            start = pl.multiple_of(t * tile, tile)
            sel = one_hot(rows_of((tile, width), start) == inner_row)
            sums[...] += dot(parts[:, pl.ds(start, tile)].astype(bf16), sel)

        total = sums[...]
        out_ref[...] = (total[0:1] * 128.0 + total[1:2]).astype(jnp.int32)

    compose(pair_ref[...], quad_ref[...], two_ref)
    compose(two_ref[...], top_ref[...], three_ref)


def fine_kernel(
    tile_ref,
    arrived_ref,
    near_ref,
    pair_ref,
    edge_in_ref,
    edge_bias_ref,
    edge_out_ref,
    node_in_ref,
    node_bias_ref,
    node_out_ref,
    gain_ref,
    fine_ref,
    side_ref,
    slots,
    dst,
    src,
    agg,
    sels,
    near_rows,
):
    count, features = fine_ref.shape
    tile = 256

    @pl.loop(0, count // tile)
    def _(t):
        here = pl.ds(pl.multiple_of(t * tile, tile), tile)
        raw = arrived_ref[here, :].astype(f32)
        present = raw[:, 0:1] < LIMIT
        rows = jnp.where(present, raw, 0.0).astype(bf16)
        slots[here, :] = rows
        to_dst = (dot(rows, edge_in_ref[0]) + edge_bias_ref[...]) * 0.5
        dst[here, :] = to_dst.astype(bf16)
        from_src = dot(rows, edge_in_ref[1]) * 0.5
        src[here, :] = jnp.where(present, from_src, AWAY).astype(bf16)

    group = 16

    @pl.loop(0, count // BLK)
    def _(b):
        start = pl.multiple_of(b * BLK, BLK)
        near = near_ref[pl.ds(start, BLK), :]
        for j in range(TPB):
            for k in range(NBR):
                at = j * NBR + k
                mask = near[:, at : at + 1] == lanes_of((BLK, BLK))
                sels[k * BLK : (k + 1) * BLK, :] = one_hot(mask)
            first = pl.multiple_of(tile_ref[b, j] * BLK, BLK)
            near_rows[j * NBR * BLK : (j + 1) * NBR * BLK, :] = dot(
                sels[...], src[pl.ds(first, BLK), :]
            ).astype(bf16)
        for r in range(0, BLK, group):
            here = dst[pl.ds(start + r, group), :]
            total = jnp.zeros((group, features), f32)
            for at in range(TPB * NBR):
                term = half_silu(here + near_rows[at * BLK + r : at * BLK + r + group, :])
                total += term.astype(f32)
            agg[pl.ds(start + r, group), :] = total.astype(bf16)

    @pl.loop(0, count // tile)
    def _(t):
        here = pl.ds(pl.multiple_of(t * tile, tile), tile)
        rows = slots[here, :]
        message = dot(agg[here, :], edge_out_ref[...]).astype(bf16)
        lifted = dot(rows, node_in_ref[0]) + dot(message, node_in_ref[1]) + node_bias_ref[...]
        hidden = half_silu(lifted * 0.5).astype(bf16)
        delta = dot(hidden, node_out_ref[...])
        scale = lax.rsqrt(jnp.mean(delta * delta, axis=-1, keepdims=True) + epsilon)
        fine = rows.astype(f32) + gain_ref[...] * (delta * scale)
        present = arrived_ref[here, 0:LANES].astype(f32)[:, 0:1] < LIMIT
        fine_ref[here, :] = jnp.where(present, fine, EMPTY).astype(bf16)

    many = 512

    @pl.loop(0, count // many)
    def _(t):
        start = pl.multiple_of(t * many, many)
        sel = picker(pair_ref, start, many, 0, count)
        side_ref[pl.ds(start, many), :] = dot(sel, fine_ref[...]).astype(bf16)


def refined(total, count, weight):
    mean_rows = total * (1.0 / jnp.maximum(count, 1.0))
    lifted = dot(mean_rows.astype(bf16), weight)
    return mean_rows + half_silu(lifted * 0.5)


def widened(column, features):
    return jnp.concatenate([column] * (features // LANES), axis=1)


def put_counts(out_ref, rows, columns):
    features = out_ref.shape[1]
    per = features // LANES
    lines = []
    for c in range(0, len(columns), per):
        lines.append(jnp.concatenate([col.T[0:1, :] for col in columns[c : c + per]], axis=1))
    which = rows_of((PAD, features))
    tail = jnp.zeros((PAD, features), f32)
    for i, line in enumerate(lines):
        tail = jnp.where(which == i, line, tail)
    out_ref[rows : rows + PAD, :] = tail.astype(bf16)


def get_count(tail, c):
    features = tail.shape[1]
    line, lane = c // features, c % features
    return spread(tail[line : line + 1, lane : lane + LANES])


def one_kernel(pick_ref, side_ref, other_ref, weight_ref, level_ref, out_ref, wide):
    count, features = level_ref.shape
    tile = 256

    @pl.loop(0, count // tile)
    def _(t):
        here = pl.ds(pl.multiple_of(t * tile, tile), tile)
        a = side_ref[here, :].astype(f32)
        b = other_ref[here, :].astype(f32)
        in_a = a[:, 0:1] < LIMIT
        in_b = b[:, 0:1] < LIMIT
        total = jnp.where(in_a, a, 0.0) + jnp.where(in_b, b, 0.0)
        marks = jnp.where(in_a, 1.0, 0.0) + jnp.where(in_b, 1.0, 0.0)
        level = refined(total, marks, weight_ref[...]).astype(bf16)
        level_ref[here, :] = level
        wide[here, 0:features] = level
        wide[here, features : features + LANES] = jnp.broadcast_to(marks, (tile, LANES)).astype(
            bf16
        )

    picked = pick_ref.shape[1]
    many = 512
    columns = []
    for start in range(0, picked, many):
        sel = picker(pick_ref, start, many, 0, count)
        got = dot(sel, wide[...])
        out_ref[start : start + many, :] = got[:, 0:features].astype(bf16)
        for c in range(0, many, LANES):
            columns.append(got[c : c + LANES, features : features + LANES])
    put_counts(out_ref, picked, columns)


def two_kernel(mine_ref, other_ref, weight_ref, out_ref):
    count = out_ref.shape[0] - PAD
    features = out_ref.shape[1]
    mine_tail = mine_ref[count : count + PAD, :].astype(f32)
    other_tail = other_ref[count : count + PAD, :].astype(f32)
    columns = []
    for c in range(0, count, LANES):
        a, b = get_count(mine_tail, c), get_count(other_tail, c)
        columns.append(a + b)
        total = widened(a, features) * mine_ref[c : c + LANES, :].astype(f32) + widened(
            b, features
        ) * other_ref[c : c + LANES, :].astype(f32)
        level = refined(total, widened(a + b, features), weight_ref[...])
        out_ref[c : c + LANES, :] = level.astype(bf16)
    put_counts(out_ref, count, columns)


def pick_kernel(place_ref, pick_ref, mine_ref, other_ref, out_ref, wide):
    count = mine_ref.shape[0] - PAD
    features = out_ref.shape[1]
    picked = pick_ref.shape[1]
    core = place_ref[0] % 2
    for piece, (ref, half) in enumerate(((mine_ref, core), (other_ref, 1 - core))):
        base = pl.multiple_of(half * count, LANES)
        wide[pl.ds(base, count), 0:features] = ref[0:count, :]
        tail = ref[count : count + PAD, :].astype(f32)
        for c in range(0, count, LANES):
            wide[pl.ds(base + c, LANES), features : features + LANES] = get_count(tail, c).astype(
                bf16
            )
    sel = picker(pick_ref, 0, picked, 0, 2 * count)
    got = dot(sel, wide[...])
    out_ref[0:picked, :] = got[:, 0:features].astype(bf16)
    put_counts(
        out_ref,
        picked,
        [got[c : c + LANES, features : features + LANES] for c in range(0, picked, LANES)],
    )


def three_kernel(all_ref, weight_ref, out_ref):
    groups = all_ref.shape[0]
    count, features = out_ref.shape
    tails = [all_ref[g, count : count + PAD, :].astype(f32) for g in range(groups)]
    for c in range(0, count, LANES):
        total, marks = 0.0, 0.0
        for g in range(groups):
            got = get_count(tails[g], c)
            marks = marks + got
            total = total + widened(got, features) * all_ref[g, c : c + LANES, :].astype(f32)
        level = refined(total, widened(marks, features), weight_ref[...])
        out_ref[c : c + LANES, :] = level.astype(bf16)


def back_kernel(last, order, place_ref, perm_ref, base_ref, *refs):
    pieces, out_ref = refs[:-1], refs[-1]
    width = perm_ref.shape[1]
    size = width // len(pieces)
    tile = 256

    @pl.loop(0, out_ref.shape[0] // tile)
    def _(t):
        start = pl.multiple_of(t * tile, tile)
        here = pl.ds(start, tile)
        base = base_ref[here, :].astype(f32)
        total = base
        for piece, flip in zip(pieces, order):
            at = (place_ref[0] % len(pieces)) ^ flip
            targets = perm_ref[:, pl.ds(pl.multiple_of(at * size, LANES), size)]
            sel = one_hot(rows_of((tile, size), start) == targets)
            total = total + dot(sel, piece[0:size, :])
        absent = 0.0 if last else EMPTY
        out_ref[here, :] = jnp.where(base[:, 0:1] < LIMIT, total, absent).astype(bf16)


def swapped(shard, flip):
    count = lax.axis_size("sub")
    return lax.ppermute(shard, "sub", [(i, i ^ flip) for i in range(count)])


def body(
    node_rows,
    owners,
    tile_src,
    neighbors,
    pool_pair,
    pool_quad,
    pool_top,
    edge_in,
    edge_bias,
    edge_out,
    node_in,
    node_bias,
    node_out,
    out_gain,
    coarse,
):
    owner_count = lax.axis_size("sub") * lax.axis_size("grp")
    slot_rows = neighbors.shape[2]
    nodes, features = node_rows.shape
    cap = slot_rows // owner_count
    me = lax.axis_index("sub")
    half, quarter = slot_rows // 2, slot_rows // 4

    def shape(rows, dtype=bf16, width=features):
        return jax.ShapeDtypeStruct((rows, width), dtype)

    placed = call(
        functools.partial(place_kernel, cap),
        shape(slot_rows),
        (owners.reshape(1, nodes), node_rows),
        flops=2 * slot_rows * nodes * features,
    )
    arrived = lax.all_to_all(
        placed.reshape(owner_count, cap, features),
        ("sub", "grp"),
        split_axis=0,
        concat_axis=0,
        tiled=True,
    ).reshape(slot_rows, features)

    pair = pool_pair.reshape(1, slot_rows)
    quad = lax.dynamic_index_in_dim(pool_quad, me // 2, 0, keepdims=False)
    top = lax.dynamic_index_in_dim(pool_top, me // 4, 0, keepdims=False)
    place = me.reshape(1).astype(jnp.int32)
    quad_half = lax.dynamic_slice_in_dim(quad, (me % 2) * half, half, 1)
    top_quarter = lax.dynamic_slice_in_dim(top, (me % 4) * quarter, quarter, 1)
    to_two, to_three = call(
        compose_kernel,
        (shape(1, jnp.int32, slot_rows), shape(1, jnp.int32, slot_rows)),
        (pair, quad, top),
        scratch=[pltpu.VMEM((8, slot_rows), f32), pltpu.VMEM((8, slot_rows), f32)],
        flops=20 * 10**9,
    )
    arrived, to_two, to_three = lax.optimization_barrier((arrived, to_two, to_three))

    fine, side = call(
        fine_kernel,
        (shape(slot_rows), shape(slot_rows)),
        (
            tile_src[0, 0],
            arrived,
            neighbors[0, 0],
            pair,
            edge_in,
            edge_bias.reshape(1, features),
            edge_out,
            node_in,
            node_bias.reshape(1, features),
            node_out,
            out_gain.reshape(1, features),
        ),
        specs=[SM] + [VM] * 10,
        scratch=[pltpu.VMEM((slot_rows, features), bf16)] * 4
        + [
            pltpu.VMEM((NBR * BLK, BLK), bf16),
            pltpu.VMEM((TPB * NBR * BLK, features), bf16),
        ],
        flops=40 * 10**9,
    )
    other = swapped(side, 1)
    wide = pltpu.VMEM((slot_rows, features + LANES), bf16)
    level_one, mine = call(
        one_kernel,
        (shape(slot_rows), shape(half + PAD)),
        (quad_half, side, other, coarse[0]),
        scratch=[wide],
        flops=4 * 10**9,
    )
    other = swapped(mine, 2)
    back = functools.partial(back_kernel, False)
    wide_flops = 2 * slot_rows * slot_rows * features
    raised = call(
        functools.partial(back, (0,)),
        shape(slot_rows),
        (place, pair, fine, level_one),
        specs=[SM] + [VM] * 3,
        flops=wide_flops,
    )
    other, raised = lax.optimization_barrier((other, raised))
    mine = call(two_kernel, shape(half + PAD), (mine, other, coarse[1]), flops=10**9)
    other = swapped(mine, 1)
    chosen = call(
        pick_kernel,
        shape(quarter + PAD),
        (place, top_quarter, mine, other),
        specs=[SM] + [VM] * 3,
        scratch=[wide],
        flops=10**9,
    )
    gathered = lax.all_gather(chosen, "grp", axis=0, tiled=False)
    raised = call(
        functools.partial(back, (0, 1)),
        shape(slot_rows),
        (place, to_two, raised, mine, other),
        specs=[SM] + [VM] * 4,
        flops=wide_flops,
    )
    gathered, raised = lax.optimization_barrier((gathered, raised))
    mine = call(three_kernel, shape(quarter), (gathered, coarse[2]), flops=10**9)
    across = swapped(mine, 2)
    return call(
        functools.partial(back_kernel, True, (0, 2, 1, 3)),
        shape(slot_rows),
        (place, to_three, raised, mine, across, swapped(mine, 1), swapped(across, 1)),
        specs=[SM] + [VM] * 6,
        flops=wide_flops,
    )


def solution(mesh):
    in_specs = (
        P(("sub", "grp"), None),
        P(("sub", "grp")),
        P("sub", "grp", None, None),
        P("sub", "grp", None, None),
        P("sub", "grp", None),
        P(None, "grp", None),
        P(None, "grp", None),
        P(),
        P(),
        P(),
        P(),
        P(),
        P(),
        P(),
        P(),
    )
    out_specs = P(("sub", "grp"), None)
    return jax.shard_map(body, mesh=mesh, in_specs=in_specs, out_specs=out_specs, check_vma=False)
```

```python
import functools

import jax
import jax.numpy as jnp
from jax import lax
from jax.experimental import pallas as pl
from jax.experimental.pallas import tpu as pltpu
from jax.sharding import PartitionSpec as P

BLK = 128
TPB = 2
NBR = 8
LANES = 128
PAD = 16
EMPTY = 16384.0
LIMIT = 8192.0
AWAY = -8192.0
epsilon = 1e-05
f32 = jnp.float32
bf16 = jnp.bfloat16

VM = pl.BlockSpec(memory_space=pltpu.VMEM)
SM = pl.BlockSpec(memory_space=pltpu.SMEM)


def call(kernel, outs, args, specs=None, scratch=(), flops=0):
    return pl.pallas_call(
        kernel,
        out_shape=outs,
        in_specs=specs or [VM] * len(args),
        out_specs=jax.tree.map(lambda _: VM, outs),
        scratch_shapes=list(scratch),
        compiler_params=pltpu.CompilerParams(vmem_limit_bytes=44 << 20),
        cost_estimate=pl.CostEstimate(flops=flops, bytes_accessed=8 << 20, transcendentals=0),
    )(*args)


def rows_of(shape, start=0):
    return lax.broadcasted_iota(jnp.int32, shape, 0) + start


def lanes_of(shape, start=0):
    return lax.broadcasted_iota(jnp.int32, shape, 1) + start


def one_hot(mask):
    return jnp.where(mask, 1.0, 0.0).astype(bf16)


def spread(row):
    return jnp.broadcast_to(row, (LANES, LANES)).T


def dot(a, b):
    return jnp.dot(a, b, preferred_element_type=f32)


def half_silu(h):
    return h + h * jnp.tanh(h)


def picker(perm_ref, first, count, start, width):
    tiles = []
    for c in range(0, count, LANES):
        column = spread(perm_ref[:, pl.ds(pl.multiple_of(first + c, LANES), LANES)])
        wide = jnp.concatenate([column] * (width // LANES), axis=1)
        tiles.append(one_hot(wide == lanes_of((LANES, width), start)))
    return jnp.concatenate(tiles, axis=0)


def place_kernel(cap, owners_ref, nodes_ref, out_ref):
    owner_row = owners_ref[...]
    nodes = owner_row.shape[1]
    position = jnp.zeros((1, nodes), f32)
    for c in range(0, nodes, LANES):
        column = spread(owners_ref[:, c : c + LANES])
        wide = jnp.concatenate([column] * (nodes // LANES), axis=1)
        shape = (LANES, nodes)
        earlier = (wide == owner_row) & (rows_of(shape, c) < lanes_of(shape))
        position += jnp.sum(jnp.where(earlier, 1.0, 0.0), axis=0, keepdims=True)
    target = owner_row * cap + position.astype(jnp.int32)
    tile = 256

    @pl.loop(0, out_ref.shape[0] // tile)
    def _(t):
        start = pl.multiple_of(t * tile, tile)
        mask = rows_of((tile, nodes), start) == target
        weight = jnp.where(mask, 1.0, 0.0)
        filled = jnp.max(weight, axis=1, keepdims=True)
        rows = dot(weight.astype(bf16), nodes_ref[...])
        out_ref[pl.ds(start, tile), :] = jnp.where(filled > 0.5, rows, EMPTY).astype(bf16)


def compose_kernel(pair_ref, quad_ref, top_ref, two_ref, three_ref, parts, sums):
    width = pair_ref.shape[1]
    tile = 256

    def compose(outer, inner_row, out_ref):
        which = rows_of((8, width))
        high = (outer >> 7).astype(f32)
        low = (outer & 127).astype(f32)
        parts[...] = jnp.where(which == 0, high, jnp.where(which == 1, low, 0.0))
        sums[...] = jnp.zeros_like(sums)

        @pl.loop(0, width // tile)
        def _(t):
            start = pl.multiple_of(t * tile, tile)
            sel = one_hot(rows_of((tile, width), start) == inner_row)
            sums[...] += dot(parts[:, pl.ds(start, tile)].astype(bf16), sel)

        total = sums[...]
        out_ref[...] = (total[0:1] * 128.0 + total[1:2]).astype(jnp.int32)

    compose(pair_ref[...], quad_ref[...], two_ref)
    compose(two_ref[...], top_ref[...], three_ref)


def fine_kernel(
    tile_ref,
    arrived_ref,
    near_ref,
    pair_ref,
    edge_in_ref,
    edge_bias_ref,
    edge_out_ref,
    node_in_ref,
    node_bias_ref,
    node_out_ref,
    gain_ref,
    fine_ref,
    side_ref,
    slots,
    dst,
    src,
    agg,
    sels,
    near_rows,
):
    count, features = fine_ref.shape
    tile = 256

    @pl.loop(0, count // tile)
    def _(t):
        here = pl.ds(pl.multiple_of(t * tile, tile), tile)
        raw = arrived_ref[here, :].astype(f32)
        present = raw[:, 0:1] < LIMIT
        rows = jnp.where(present, raw, 0.0).astype(bf16)
        slots[here, :] = rows
        to_dst = (dot(rows, edge_in_ref[0]) + edge_bias_ref[...]) * 0.5
        dst[here, :] = to_dst.astype(bf16)
        from_src = dot(rows, edge_in_ref[1]) * 0.5
        src[here, :] = jnp.where(present, from_src, AWAY).astype(bf16)

    group = 16

    @pl.loop(0, count // BLK)
    def _(b):
        start = pl.multiple_of(b * BLK, BLK)
        near = near_ref[pl.ds(start, BLK), :]
        for j in range(TPB):
            for k in range(NBR):
                at = j * NBR + k
                mask = near[:, at : at + 1] == lanes_of((BLK, BLK))
                sels[k * BLK : (k + 1) * BLK, :] = one_hot(mask)
            first = pl.multiple_of(tile_ref[b, j] * BLK, BLK)
            near_rows[j * NBR * BLK : (j + 1) * NBR * BLK, :] = dot(
                sels[...], src[pl.ds(first, BLK), :]
            )
        for r in range(0, BLK, group):
            here = dst[pl.ds(start + r, group), :].astype(f32)
            total = jnp.zeros((group, features), f32)
            for at in range(TPB * NBR):
                total += half_silu(here + near_rows[at * BLK + r : at * BLK + r + group, :])
            agg[pl.ds(start + r, group), :] = total.astype(bf16)

    @pl.loop(0, count // tile)
    def _(t):
        here = pl.ds(pl.multiple_of(t * tile, tile), tile)
        rows = slots[here, :]
        message = dot(agg[here, :], edge_out_ref[...]).astype(bf16)
        lifted = dot(rows, node_in_ref[0]) + dot(message, node_in_ref[1]) + node_bias_ref[...]
        hidden = half_silu(lifted * 0.5).astype(bf16)
        delta = dot(hidden, node_out_ref[...])
        scale = lax.rsqrt(jnp.mean(delta * delta, axis=-1, keepdims=True) + epsilon)
        fine = rows.astype(f32) + gain_ref[...] * (delta * scale)
        present = arrived_ref[here, 0:LANES].astype(f32)[:, 0:1] < LIMIT
        fine_ref[here, :] = jnp.where(present, fine, EMPTY).astype(bf16)

    many = 512

    @pl.loop(0, count // many)
    def _(t):
        start = pl.multiple_of(t * many, many)
        sel = picker(pair_ref, start, many, 0, count)
        side_ref[pl.ds(start, many), :] = dot(sel, fine_ref[...]).astype(bf16)


def refined(total, count, weight):
    mean_rows = total * (1.0 / jnp.maximum(count, 1.0))
    lifted = dot(mean_rows.astype(bf16), weight)
    return mean_rows + half_silu(lifted * 0.5)


def widened(column, features):
    return jnp.concatenate([column] * (features // LANES), axis=1)


def put_counts(out_ref, rows, columns):
    features = out_ref.shape[1]
    per = features // LANES
    lines = []
    for c in range(0, len(columns), per):
        parts = [col.T[0:1, :] for col in columns[c : c + per]]
        parts += [jnp.zeros((1, LANES), f32)] * (per - len(parts))
        lines.append(jnp.concatenate(parts, axis=1))
    which = rows_of((PAD, features))
    tail = jnp.zeros((PAD, features), f32)
    for i, line in enumerate(lines):
        tail = jnp.where(which == i, line, tail)
    out_ref[rows : rows + PAD, :] = tail.astype(bf16)


def get_count(tail, c):
    features = tail.shape[1]
    line, lane = c // features, c % features
    return spread(tail[line : line + 1, lane : lane + LANES])


def one_kernel(pick_ref, side_ref, other_ref, weight_ref, level_ref, out_ref, wide):
    count, features = level_ref.shape
    tile = 256

    @pl.loop(0, count // tile)
    def _(t):
        here = pl.ds(pl.multiple_of(t * tile, tile), tile)
        a = side_ref[here, :].astype(f32)
        b = other_ref[here, :].astype(f32)
        in_a = a[:, 0:1] < LIMIT
        in_b = b[:, 0:1] < LIMIT
        total = jnp.where(in_a, a, 0.0) + jnp.where(in_b, b, 0.0)
        marks = jnp.where(in_a, 1.0, 0.0) + jnp.where(in_b, 1.0, 0.0)
        level = refined(total, marks, weight_ref[...]).astype(bf16)
        level_ref[here, :] = level
        wide[here, 0:features] = level
        wide[here, features : features + LANES] = jnp.broadcast_to(marks, (tile, LANES)).astype(
            bf16
        )

    picked = pick_ref.shape[1]
    many = 512
    columns = []
    for start in range(0, picked, many):
        sel = picker(pick_ref, start, many, 0, count)
        got = dot(sel, wide[...])
        out_ref[start : start + many, :] = got[:, 0:features].astype(bf16)
        for c in range(0, many, LANES):
            columns.append(got[c : c + LANES, features : features + LANES])
    put_counts(out_ref, picked, columns)


def two_kernel(mine_ref, other_ref, weight_ref, out_ref):
    count = out_ref.shape[0] - PAD
    features = out_ref.shape[1]
    mine_tail = mine_ref[count : count + PAD, :].astype(f32)
    other_tail = other_ref[count : count + PAD, :].astype(f32)
    columns = []
    for c in range(0, count, LANES):
        a, b = get_count(mine_tail, c), get_count(other_tail, c)
        columns.append(a + b)
        total = widened(a, features) * mine_ref[c : c + LANES, :].astype(f32) + widened(
            b, features
        ) * other_ref[c : c + LANES, :].astype(f32)
        level = refined(total, widened(a + b, features), weight_ref[...])
        out_ref[c : c + LANES, :] = level.astype(bf16)
    put_counts(out_ref, count, columns)


def pick_kernel(groups, place_ref, pick_ref, mine_ref, other_ref, out_ref, wide):
    count = mine_ref.shape[0] - PAD
    features = out_ref.shape[1]
    picked = pick_ref.shape[1]
    core = place_ref[0] % 2
    for piece, (ref, half) in enumerate(((mine_ref, core), (other_ref, 1 - core))):
        base = pl.multiple_of(half * count, LANES)
        wide[pl.ds(base, count), 0:features] = ref[0:count, :]
        tail = ref[count : count + PAD, :].astype(f32)
        for c in range(0, count, LANES):
            wide[pl.ds(base + c, LANES), features : features + LANES] = get_count(tail, c).astype(
                bf16
            )
    sel = picker(pick_ref, 0, picked, 0, 2 * count)
    got = dot(sel, wide[...])
    piece = picked // groups
    for g in range(groups):
        base, first = g * (piece + PAD), g * piece
        out_ref[base : base + piece, :] = got[first : first + piece, 0:features].astype(bf16)
        columns = [
            got[first + c : first + c + LANES, features : features + LANES]
            for c in range(0, piece, LANES)
        ]
        put_counts(out_ref, base + piece, columns)


def top_kernel(groups, parts_ref, weight_ref, level_ref, inbox, sends, receives):
    packet = parts_ref.shape[0] // groups
    piece = packet - PAD
    features = level_ref.shape[1]
    a, g = lax.axis_index("sub"), lax.axis_index("grp")
    across = a + 2 - 4 * ((a // 2) % 2)
    core = a + 1 - 2 * (a % 2)
    others = [lax.rem(g + d, groups) for d in range(1, groups)]
    peers = [{"grp": t} for t in others] + [{"sub": across}, {"sub": core}]
    barrier = pltpu.get_barrier_semaphore()
    for peer in peers:
        pl.semaphore_signal(barrier, inc=1, device_id=peer, device_id_type=pl.DeviceIdType.MESH)
    pl.semaphore_wait(barrier, len(peers))

    def packet_of(t):
        return pl.ds(pl.multiple_of(t * packet, PAD), packet)

    def piece_of(sub, group):
        return pl.ds(pl.multiple_of(((sub % 4) * groups + group) * piece, piece), piece)

    def send(stage, d, source, target, peer):
        copy = pltpu.make_async_remote_copy(
            src_ref=source,
            dst_ref=target,
            send_sem=sends.at[stage, d],
            recv_sem=receives.at[stage, d],
            device_id=peer,
            device_id_type=pl.DeviceIdType.MESH,
        )
        copy.start()
        return copy

    def relay(stage, d, rows, peer):
        return send(stage, d, level_ref.at[rows, :], level_ref.at[rows, :], peer)

    first = [
        send(0, d, parts_ref.at[packet_of(t), :], inbox.at[d], {"grp": t})
        for d, t in enumerate(others)
    ]
    own = pl.multiple_of(g * packet, PAD)
    for copy in first:
        copy.wait_recv()
    terms = [lambda at, size: parts_ref[pl.ds(own + at, size), :].astype(f32)]
    for d in range(groups - 1):
        terms.append(lambda at, size, d=d: inbox[d, at : at + size, :].astype(f32))
    tails = [term(piece, PAD) for term in terms]
    base = pl.multiple_of(((a % 4) * groups + g) * piece, piece)
    for c in range(0, piece, LANES):
        total, marks = 0.0, 0.0
        for term, tail in zip(terms, tails):
            got = get_count(tail, c)
            marks = marks + got
            total = total + widened(got, features) * term(c, LANES)
        level = refined(total, widened(marks, features), weight_ref[...])
        level_ref[pl.ds(base + c, LANES), :] = level.astype(bf16)

    mine = piece_of(a, g)
    pieces = [mine] + [piece_of(a, lax.rem(g + groups - d, groups)) for d in range(1, groups)]
    theirs = [piece_of(across, lax.rem(g + groups - d, groups)) for d in range(groups)]
    over_x = [relay(2, 0, mine, {"sub": across})]
    over_z = [relay(1, d, mine, {"grp": t}) for d, t in enumerate(others)]
    over_core = [relay(3, 0, mine, {"sub": core})]
    for d in range(1, groups):
        over_z[d - 1].wait_recv()
        over_x.append(relay(2, d, pieces[d], {"sub": across}))
        over_core.append(relay(3, d, pieces[d], {"sub": core}))
    relayed = []
    for d in range(groups):
        over_x[d].wait_recv()
        relayed.append(relay(4, d, theirs[d], {"sub": core}))
    for copy in over_core + relayed:
        copy.wait_recv()
    for copy in first + over_z + over_x + over_core + relayed:
        copy.wait_send()


def back_kernel(last, order, place_ref, perm_ref, base_ref, *refs):
    pieces, out_ref = refs[:-1], refs[-1]
    width = perm_ref.shape[1]
    size = width // len(pieces)
    tile = 256

    @pl.loop(0, out_ref.shape[0] // tile)
    def _(t):
        start = pl.multiple_of(t * tile, tile)
        here = pl.ds(start, tile)
        base = base_ref[here, :].astype(f32)
        total = base
        for piece, flip in zip(pieces, order):
            at = (place_ref[0] % len(pieces)) ^ flip
            targets = perm_ref[:, pl.ds(pl.multiple_of(at * size, LANES), size)]
            sel = one_hot(rows_of((tile, size), start) == targets)
            total = total + dot(sel, piece[0:size, :])
        absent = 0.0 if last else EMPTY
        out_ref[here, :] = jnp.where(base[:, 0:1] < LIMIT, total, absent).astype(bf16)


def swapped(shard, flip):
    count = lax.axis_size("sub")
    return lax.ppermute(shard, "sub", [(i, i ^ flip) for i in range(count)])


def body(
    node_rows,
    owners,
    tile_src,
    neighbors,
    pool_pair,
    pool_quad,
    pool_top,
    edge_in,
    edge_bias,
    edge_out,
    node_in,
    node_bias,
    node_out,
    out_gain,
    coarse,
):
    owner_count = lax.axis_size("sub") * lax.axis_size("grp")
    slot_rows = neighbors.shape[2]
    nodes, features = node_rows.shape
    cap = slot_rows // owner_count
    me = lax.axis_index("sub")
    half, quarter = slot_rows // 2, slot_rows // 4

    def shape(rows, dtype=bf16, width=features):
        return jax.ShapeDtypeStruct((rows, width), dtype)

    placed = call(
        functools.partial(place_kernel, cap),
        shape(slot_rows),
        (owners.reshape(1, nodes), node_rows),
        flops=2 * slot_rows * nodes * features,
    )
    arrived = lax.all_to_all(
        placed.reshape(owner_count, cap, features),
        ("sub", "grp"),
        split_axis=0,
        concat_axis=0,
        tiled=True,
    ).reshape(slot_rows, features)

    pair = pool_pair.reshape(1, slot_rows)
    quad = lax.dynamic_index_in_dim(pool_quad, me // 2, 0, keepdims=False)
    top = lax.dynamic_index_in_dim(pool_top, me // 4, 0, keepdims=False)
    place = me.reshape(1).astype(jnp.int32)
    quad_half = lax.dynamic_slice_in_dim(quad, (me % 2) * half, half, 1)
    top_quarter = lax.dynamic_slice_in_dim(top, (me % 4) * quarter, quarter, 1)
    to_two, to_three = call(
        compose_kernel,
        (shape(1, jnp.int32, slot_rows), shape(1, jnp.int32, slot_rows)),
        (pair, quad, top),
        scratch=[pltpu.VMEM((8, slot_rows), f32), pltpu.VMEM((8, slot_rows), f32)],
        flops=20 * 10**9,
    )
    arrived, to_two, to_three = lax.optimization_barrier((arrived, to_two, to_three))

    fine, side = call(
        fine_kernel,
        (shape(slot_rows), shape(slot_rows)),
        (
            tile_src[0, 0],
            arrived,
            neighbors[0, 0],
            pair,
            edge_in,
            edge_bias.reshape(1, features),
            edge_out,
            node_in,
            node_bias.reshape(1, features),
            node_out,
            out_gain.reshape(1, features),
        ),
        specs=[SM] + [VM] * 10,
        scratch=[pltpu.VMEM((slot_rows, features), bf16)] * 4
        + [
            pltpu.VMEM((NBR * BLK, BLK), bf16),
            pltpu.VMEM((TPB * NBR * BLK, features), f32),
        ],
        flops=40 * 10**9,
    )
    other = swapped(side, 1)
    wide = pltpu.VMEM((slot_rows, features + LANES), bf16)
    level_one, mine = call(
        one_kernel,
        (shape(slot_rows), shape(half + PAD)),
        (quad_half, side, other, coarse[0]),
        scratch=[wide],
        flops=4 * 10**9,
    )
    other = swapped(mine, 2)
    back = functools.partial(back_kernel, False)
    wide_flops = 2 * slot_rows * slot_rows * features
    raised = call(
        functools.partial(back, (0,)),
        shape(slot_rows),
        (place, pair, fine, level_one),
        specs=[SM] + [VM] * 3,
        flops=wide_flops,
    )
    other, raised = lax.optimization_barrier((other, raised))
    mine = call(two_kernel, shape(half + PAD), (mine, other, coarse[1]), flops=10**9)
    other = swapped(mine, 1)
    groups = lax.axis_size("grp")
    packet = quarter // groups + PAD
    chosen = call(
        functools.partial(pick_kernel, groups),
        shape(groups * packet),
        (place, top_quarter, mine, other),
        specs=[SM] + [VM] * 3,
        scratch=[wide],
        flops=10**9,
    )
    level_three = pl.pallas_call(
        functools.partial(top_kernel, groups),
        out_shape=shape(slot_rows),
        in_specs=[VM] * 2,
        out_specs=VM,
        scratch_shapes=[
            pltpu.VMEM((groups - 1, packet, features), bf16),
            pltpu.SemaphoreType.DMA((5, groups)),
            pltpu.SemaphoreType.DMA((5, groups)),
        ],
        compiler_params=pltpu.CompilerParams(collective_id=0, has_side_effects=True),
    )(chosen, coarse[2])
    raised = call(
        functools.partial(back, (0, 1)),
        shape(slot_rows),
        (place, to_two, raised, mine, other),
        specs=[SM] + [VM] * 4,
        flops=wide_flops,
    )
    return call(
        functools.partial(back_kernel, True, (0,)),
        shape(slot_rows),
        (place, to_three, raised, level_three),
        specs=[SM] + [VM] * 3,
        flops=wide_flops,
    )


def solution(mesh):
    in_specs = (
        P(("sub", "grp"), None),
        P(("sub", "grp")),
        P("sub", "grp", None, None),
        P("sub", "grp", None, None),
        P("sub", "grp", None),
        P(None, "grp", None),
        P(None, "grp", None),
        P(),
        P(),
        P(),
        P(),
        P(),
        P(),
        P(),
        P(),
    )
    out_specs = P(("sub", "grp"), None)
    return jax.shard_map(body, mesh=mesh, in_specs=in_specs, out_specs=out_specs, check_vma=False)
```

```python
import functools

import jax
import jax.numpy as jnp
from jax import lax
from jax.experimental import pallas as pl
from jax.experimental.pallas import tpu as pltpu
from jax.sharding import PartitionSpec as P

BLK = 128
TPB = 2
NBR = 8
LANES = 128
PAD = 16
EMPTY = 16384.0
LIMIT = 8192.0
AWAY = -8192.0
epsilon = 1e-05
f32 = jnp.float32
bf16 = jnp.bfloat16

VM = pl.BlockSpec(memory_space=pltpu.VMEM)
SM = pl.BlockSpec(memory_space=pltpu.SMEM)


def call(kernel, outs, args, specs=None, scratch=(), flops=0):
    return pl.pallas_call(
        kernel,
        out_shape=outs,
        in_specs=specs or [VM] * len(args),
        out_specs=jax.tree.map(lambda _: VM, outs),
        scratch_shapes=list(scratch),
        compiler_params=pltpu.CompilerParams(vmem_limit_bytes=44 << 20),
        cost_estimate=pl.CostEstimate(flops=flops, bytes_accessed=8 << 20, transcendentals=0),
    )(*args)


def rows_of(shape, start=0):
    return lax.broadcasted_iota(jnp.int32, shape, 0) + start


def lanes_of(shape, start=0):
    return lax.broadcasted_iota(jnp.int32, shape, 1) + start


def one_hot(mask):
    return jnp.where(mask, 1.0, 0.0).astype(bf16)


def spread(row):
    return jnp.broadcast_to(row, (LANES, LANES)).T


def dot(a, b):
    return jnp.dot(a, b, preferred_element_type=f32)


def half_silu(h):
    return h + h * jnp.tanh(h)


def picker(perm_ref, first, count, start, width):
    tiles = []
    for c in range(0, count, LANES):
        column = spread(perm_ref[:, pl.ds(pl.multiple_of(first + c, LANES), LANES)])
        wide = jnp.concatenate([column] * (width // LANES), axis=1)
        tiles.append(one_hot(wide == lanes_of((LANES, width), start)))
    return jnp.concatenate(tiles, axis=0)


def place_kernel(cap, owners_ref, nodes_ref, out_ref):
    owner_row = owners_ref[...]
    nodes = owner_row.shape[1]
    position = jnp.zeros((1, nodes), f32)
    for c in range(0, nodes, LANES):
        column = spread(owners_ref[:, c : c + LANES])
        wide = jnp.concatenate([column] * (nodes // LANES), axis=1)
        shape = (LANES, nodes)
        earlier = (wide == owner_row) & (rows_of(shape, c) < lanes_of(shape))
        position += jnp.sum(jnp.where(earlier, 1.0, 0.0), axis=0, keepdims=True)
    target = owner_row * cap + position.astype(jnp.int32)
    tile = 256

    @pl.loop(0, out_ref.shape[0] // tile)
    def _(t):
        start = pl.multiple_of(t * tile, tile)
        mask = rows_of((tile, nodes), start) == target
        weight = jnp.where(mask, 1.0, 0.0)
        filled = jnp.max(weight, axis=1, keepdims=True)
        rows = dot(weight.astype(bf16), nodes_ref[...])
        out_ref[pl.ds(start, tile), :] = jnp.where(filled > 0.5, rows, EMPTY).astype(bf16)


def compose_kernel(pair_ref, quad_ref, top_ref, two_ref, three_ref, parts, sums):
    width = pair_ref.shape[1]
    tile = 256

    def compose(outer, inner_row, out_ref):
        which = rows_of((8, width))
        high = (outer >> 7).astype(f32)
        low = (outer & 127).astype(f32)
        parts[...] = jnp.where(which == 0, high, jnp.where(which == 1, low, 0.0))
        sums[...] = jnp.zeros_like(sums)

        @pl.loop(0, width // tile)
        def _(t):
            start = pl.multiple_of(t * tile, tile)
            sel = one_hot(rows_of((tile, width), start) == inner_row)
            sums[...] += dot(parts[:, pl.ds(start, tile)].astype(bf16), sel)

        total = sums[...]
        out_ref[...] = (total[0:1] * 128.0 + total[1:2]).astype(jnp.int32)

    compose(pair_ref[...], quad_ref[...], two_ref)
    compose(two_ref[...], top_ref[...], three_ref)


def fine_kernel(
    tile_ref,
    arrived_ref,
    near_ref,
    pair_ref,
    edge_in_ref,
    edge_bias_ref,
    edge_out_ref,
    node_in_ref,
    node_bias_ref,
    node_out_ref,
    gain_ref,
    fine_ref,
    side_ref,
    slots,
    dst,
    src,
    agg,
    sels_a,
    sels_b,
    near_a,
    near_b,
):
    count, features = fine_ref.shape
    tile = 256

    @pl.loop(0, count // tile)
    def _(t):
        here = pl.ds(pl.multiple_of(t * tile, tile), tile)
        raw = arrived_ref[here, :].astype(f32)
        present = raw[:, 0:1] < LIMIT
        rows = jnp.where(present, raw, 0.0).astype(bf16)
        slots[here, :] = rows
        to_dst = (dot(rows, edge_in_ref[0]) + edge_bias_ref[...]) * 0.5
        dst[here, :] = to_dst.astype(bf16)
        from_src = dot(rows, edge_in_ref[1]) * 0.5
        src[here, :] = jnp.where(present, from_src, AWAY).astype(bf16)

    group = 16
    blocks = count // BLK

    def gather(b, sels, near_rows):
        near = near_ref[pl.ds(pl.multiple_of(b * BLK, BLK), BLK), :]
        for j in range(TPB):
            first = pl.multiple_of(tile_ref[b, j] * BLK, BLK)
            for k in range(NBR):
                at = j * NBR + k
                mask = near[:, at : at + 1] == lanes_of((BLK, BLK))
                sels[at * BLK : (at + 1) * BLK, :] = one_hot(mask)
            part = slice(j * NBR * BLK, (j + 1) * NBR * BLK)
            near_rows[part, :] = dot(sels[part, :], src[pl.ds(first, BLK), :])

    def sum_edges(b, near_rows):
        start = pl.multiple_of(b * BLK, BLK)
        for r in range(0, BLK, group):
            here = dst[pl.ds(start + r, group), :].astype(f32)
            total = jnp.zeros((group, features), f32)
            for at in range(TPB * NBR):
                total += half_silu(here + near_rows[at * BLK + r : at * BLK + r + group, :])
            agg[pl.ds(start + r, group), :] = total.astype(bf16)

    gather(0, sels_a, near_a)

    @pl.loop(0, blocks // 2)
    def _(i):
        gather(2 * i + 1, sels_b, near_b)
        sum_edges(2 * i, near_a)
        gather(jnp.minimum(2 * i + 2, blocks - 1), sels_a, near_a)
        sum_edges(2 * i + 1, near_b)

    @pl.loop(0, count // tile)
    def _(t):
        here = pl.ds(pl.multiple_of(t * tile, tile), tile)
        rows = slots[here, :]
        message = dot(agg[here, :], edge_out_ref[...]).astype(bf16)
        lifted = dot(rows, node_in_ref[0]) + dot(message, node_in_ref[1]) + node_bias_ref[...]
        hidden = half_silu(lifted * 0.5).astype(bf16)
        delta = dot(hidden, node_out_ref[...])
        scale = lax.rsqrt(jnp.mean(delta * delta, axis=-1, keepdims=True) + epsilon)
        fine = rows.astype(f32) + gain_ref[...] * (delta * scale)
        present = arrived_ref[here, 0:LANES].astype(f32)[:, 0:1] < LIMIT
        fine_ref[here, :] = jnp.where(present, fine, EMPTY).astype(bf16)

    many = 512

    @pl.loop(0, count // many)
    def _(t):
        start = pl.multiple_of(t * many, many)
        sel = picker(pair_ref, start, many, 0, count)
        side_ref[pl.ds(start, many), :] = dot(sel, fine_ref[...]).astype(bf16)


def refined(total, count, weight):
    mean_rows = total * (1.0 / jnp.maximum(count, 1.0))
    lifted = dot(mean_rows.astype(bf16), weight)
    return mean_rows + half_silu(lifted * 0.5)


def widened(column, features):
    return jnp.concatenate([column] * (features // LANES), axis=1)


def put_counts(out_ref, rows, columns):
    features = out_ref.shape[1]
    per = features // LANES
    lines = []
    for c in range(0, len(columns), per):
        parts = [col.T[0:1, :] for col in columns[c : c + per]]
        parts += [jnp.zeros((1, LANES), f32)] * (per - len(parts))
        lines.append(jnp.concatenate(parts, axis=1))
    which = rows_of((PAD, features))
    tail = jnp.zeros((PAD, features), f32)
    for i, line in enumerate(lines):
        tail = jnp.where(which == i, line, tail)
    out_ref[rows : rows + PAD, :] = tail.astype(bf16)


def get_count(tail, c):
    features = tail.shape[1]
    line, lane = c // features, c % features
    return spread(tail[line : line + 1, lane : lane + LANES])


def one_kernel(pick_ref, side_ref, other_ref, weight_ref, level_ref, out_ref, wide):
    count, features = level_ref.shape
    tile = 256

    @pl.loop(0, count // tile)
    def _(t):
        here = pl.ds(pl.multiple_of(t * tile, tile), tile)
        a = side_ref[here, :].astype(f32)
        b = other_ref[here, :].astype(f32)
        in_a = a[:, 0:1] < LIMIT
        in_b = b[:, 0:1] < LIMIT
        total = jnp.where(in_a, a, 0.0) + jnp.where(in_b, b, 0.0)
        marks = jnp.where(in_a, 1.0, 0.0) + jnp.where(in_b, 1.0, 0.0)
        level = refined(total, marks, weight_ref[...]).astype(bf16)
        level_ref[here, :] = level
        wide[here, 0:features] = level
        wide[here, features : features + LANES] = jnp.broadcast_to(marks, (tile, LANES)).astype(
            bf16
        )

    picked = pick_ref.shape[1]
    many = 512
    columns = []
    for start in range(0, picked, many):
        sel = picker(pick_ref, start, many, 0, count)
        got = dot(sel, wide[...])
        out_ref[start : start + many, :] = got[:, 0:features].astype(bf16)
        for c in range(0, many, LANES):
            columns.append(got[c : c + LANES, features : features + LANES])
    put_counts(out_ref, picked, columns)


def two_kernel(mine_ref, other_ref, weight_ref, out_ref):
    count = out_ref.shape[0] - PAD
    features = out_ref.shape[1]
    mine_tail = mine_ref[count : count + PAD, :].astype(f32)
    other_tail = other_ref[count : count + PAD, :].astype(f32)
    columns = []
    for c in range(0, count, LANES):
        a, b = get_count(mine_tail, c), get_count(other_tail, c)
        columns.append(a + b)
        total = widened(a, features) * mine_ref[c : c + LANES, :].astype(f32) + widened(
            b, features
        ) * other_ref[c : c + LANES, :].astype(f32)
        level = refined(total, widened(a + b, features), weight_ref[...])
        out_ref[c : c + LANES, :] = level.astype(bf16)
    put_counts(out_ref, count, columns)


def pick_kernel(groups, place_ref, pick_ref, mine_ref, other_ref, out_ref, wide):
    count = mine_ref.shape[0] - PAD
    features = out_ref.shape[1]
    picked = pick_ref.shape[1]
    core = place_ref[0] % 2
    for piece, (ref, half) in enumerate(((mine_ref, core), (other_ref, 1 - core))):
        base = pl.multiple_of(half * count, LANES)
        wide[pl.ds(base, count), 0:features] = ref[0:count, :]
        tail = ref[count : count + PAD, :].astype(f32)
        for c in range(0, count, LANES):
            wide[pl.ds(base + c, LANES), features : features + LANES] = get_count(tail, c).astype(
                bf16
            )
    sel = picker(pick_ref, 0, picked, 0, 2 * count)
    got = dot(sel, wide[...])
    piece = picked // groups
    for g in range(groups):
        base, first = g * (piece + PAD), g * piece
        out_ref[base : base + piece, :] = got[first : first + piece, 0:features].astype(bf16)
        columns = [
            got[first + c : first + c + LANES, features : features + LANES]
            for c in range(0, piece, LANES)
        ]
        put_counts(out_ref, base + piece, columns)


def top_kernel(groups, parts_ref, weight_ref, level_ref, inbox, sends, receives):
    packet = parts_ref.shape[0] // groups
    piece = packet - PAD
    features = level_ref.shape[1]
    a, g = lax.axis_index("sub"), lax.axis_index("grp")
    across = a + 2 - 4 * ((a // 2) % 2)
    core = a + 1 - 2 * (a % 2)
    others = [lax.rem(g + d, groups) for d in range(1, groups)]
    peers = [{"grp": t} for t in others] + [{"sub": across}, {"sub": core}]
    barrier = pltpu.get_barrier_semaphore()
    for peer in peers:
        pl.semaphore_signal(barrier, inc=1, device_id=peer, device_id_type=pl.DeviceIdType.MESH)
    pl.semaphore_wait(barrier, len(peers))

    def packet_of(t):
        return pl.ds(pl.multiple_of(t * packet, PAD), packet)

    def piece_of(sub, group):
        return pl.ds(pl.multiple_of(((sub % 4) * groups + group) * piece, piece), piece)

    def send(stage, d, source, target, peer):
        copy = pltpu.make_async_remote_copy(
            src_ref=source,
            dst_ref=target,
            send_sem=sends.at[stage, d],
            recv_sem=receives.at[stage, d],
            device_id=peer,
            device_id_type=pl.DeviceIdType.MESH,
        )
        copy.start()
        return copy

    def relay(stage, d, rows, peer):
        return send(stage, d, level_ref.at[rows, :], level_ref.at[rows, :], peer)

    first = [
        send(0, d, parts_ref.at[packet_of(t), :], inbox.at[d], {"grp": t})
        for d, t in enumerate(others)
    ]
    own = pl.multiple_of(g * packet, PAD)
    for copy in first:
        copy.wait_recv()
    terms = [lambda at, size: parts_ref[pl.ds(own + at, size), :].astype(f32)]
    for d in range(groups - 1):
        terms.append(lambda at, size, d=d: inbox[d, at : at + size, :].astype(f32))
    tails = [term(piece, PAD) for term in terms]
    base = pl.multiple_of(((a % 4) * groups + g) * piece, piece)
    for c in range(0, piece, LANES):
        total, marks = 0.0, 0.0
        for term, tail in zip(terms, tails):
            got = get_count(tail, c)
            marks = marks + got
            total = total + widened(got, features) * term(c, LANES)
        level = refined(total, widened(marks, features), weight_ref[...])
        level_ref[pl.ds(base + c, LANES), :] = level.astype(bf16)

    mine = piece_of(a, g)
    pieces = [mine] + [piece_of(a, lax.rem(g + groups - d, groups)) for d in range(1, groups)]
    theirs = [piece_of(across, lax.rem(g + groups - d, groups)) for d in range(groups)]
    over_x = [relay(2, 0, mine, {"sub": across})]
    over_z = [relay(1, d, mine, {"grp": t}) for d, t in enumerate(others)]
    over_core = [relay(3, 0, mine, {"sub": core})]
    for d in range(1, groups):
        over_z[d - 1].wait_recv()
        over_x.append(relay(2, d, pieces[d], {"sub": across}))
        over_core.append(relay(3, d, pieces[d], {"sub": core}))
    relayed = []
    for d in range(groups):
        over_x[d].wait_recv()
        relayed.append(relay(4, d, theirs[d], {"sub": core}))
    for copy in over_core + relayed:
        copy.wait_recv()
    for copy in first + over_z + over_x + over_core + relayed:
        copy.wait_send()


def sent(perm_ref, first, rows, start, tile):
    size = rows.shape[0]
    targets = perm_ref[:, pl.ds(first, size)]
    return dot(one_hot(rows_of((tile, size), start) == targets), rows)


def back_kernel(perm_ref, base_ref, level_ref, out_ref):
    tile = 256

    @pl.loop(0, out_ref.shape[0] // tile)
    def _(t):
        start = pl.multiple_of(t * tile, tile)
        here = pl.ds(start, tile)
        base = base_ref[here, :].astype(f32)
        total = base + sent(perm_ref, 0, level_ref[...], start, tile)
        out_ref[here, :] = jnp.where(base[:, 0:1] < LIMIT, total, EMPTY).astype(bf16)


def last_kernel(
    place_ref, two_ref, three_ref, base_ref, mine_ref, other_ref, level_ref, out_ref
):
    tile = 256
    half = level_ref.shape[0] // 2
    core = place_ref[0] % 2
    mine_at = pl.multiple_of(core * half, LANES)
    other_at = pl.multiple_of((1 - core) * half, LANES)

    @pl.loop(0, out_ref.shape[0] // tile)
    def _(t):
        start = pl.multiple_of(t * tile, tile)
        here = pl.ds(start, tile)
        base = base_ref[here, :].astype(f32)
        total = base + sent(three_ref, 0, level_ref[...], start, tile)
        total += sent(two_ref, mine_at, mine_ref[0:half, :], start, tile)
        total += sent(two_ref, other_at, other_ref[0:half, :], start, tile)
        out_ref[here, :] = jnp.where(base[:, 0:1] < LIMIT, total, 0.0).astype(bf16)


def swapped(shard, flip):
    count = lax.axis_size("sub")
    return lax.ppermute(shard, "sub", [(i, i ^ flip) for i in range(count)])


def body(
    node_rows,
    owners,
    tile_src,
    neighbors,
    pool_pair,
    pool_quad,
    pool_top,
    edge_in,
    edge_bias,
    edge_out,
    node_in,
    node_bias,
    node_out,
    out_gain,
    coarse,
):
    owner_count = lax.axis_size("sub") * lax.axis_size("grp")
    slot_rows = neighbors.shape[2]
    nodes, features = node_rows.shape
    cap = slot_rows // owner_count
    me = lax.axis_index("sub")
    half, quarter = slot_rows // 2, slot_rows // 4

    def shape(rows, dtype=bf16, width=features):
        return jax.ShapeDtypeStruct((rows, width), dtype)

    placed = call(
        functools.partial(place_kernel, cap),
        shape(slot_rows),
        (owners.reshape(1, nodes), node_rows),
        flops=2 * slot_rows * nodes * features,
    )
    arrived = lax.all_to_all(
        placed.reshape(owner_count, cap, features),
        ("sub", "grp"),
        split_axis=0,
        concat_axis=0,
        tiled=True,
    ).reshape(slot_rows, features)

    pair = pool_pair.reshape(1, slot_rows)
    quad = lax.dynamic_index_in_dim(pool_quad, me // 2, 0, keepdims=False)
    top = lax.dynamic_index_in_dim(pool_top, me // 4, 0, keepdims=False)
    place = me.reshape(1).astype(jnp.int32)
    quad_half = lax.dynamic_slice_in_dim(quad, (me % 2) * half, half, 1)
    top_quarter = lax.dynamic_slice_in_dim(top, (me % 4) * quarter, quarter, 1)
    to_two, to_three = call(
        compose_kernel,
        (shape(1, jnp.int32, slot_rows), shape(1, jnp.int32, slot_rows)),
        (pair, quad, top),
        scratch=[pltpu.VMEM((8, slot_rows), f32), pltpu.VMEM((8, slot_rows), f32)],
        flops=20 * 10**9,
    )
    arrived, to_two, to_three = lax.optimization_barrier((arrived, to_two, to_three))

    fine, side = call(
        fine_kernel,
        (shape(slot_rows), shape(slot_rows)),
        (
            tile_src[0, 0],
            arrived,
            neighbors[0, 0],
            pair,
            edge_in,
            edge_bias.reshape(1, features),
            edge_out,
            node_in,
            node_bias.reshape(1, features),
            node_out,
            out_gain.reshape(1, features),
        ),
        specs=[SM] + [VM] * 10,
        scratch=[pltpu.VMEM((slot_rows, features), bf16)] * 4
        + [
            pltpu.VMEM((TPB * NBR * BLK, BLK), bf16),
            pltpu.VMEM((TPB * NBR * BLK, BLK), bf16),
            pltpu.VMEM((TPB * NBR * BLK, features), f32),
            pltpu.VMEM((TPB * NBR * BLK, features), f32),
        ],
        flops=40 * 10**9,
    )
    other = swapped(side, 1)
    wide = pltpu.VMEM((slot_rows, features + LANES), bf16)
    level_one, mine = call(
        one_kernel,
        (shape(slot_rows), shape(half + PAD)),
        (quad_half, side, other, coarse[0]),
        scratch=[wide],
        flops=4 * 10**9,
    )
    other = swapped(mine, 2)
    wide_flops = 2 * slot_rows * slot_rows * features
    raised = call(
        back_kernel, shape(slot_rows), (pair, fine, level_one), flops=wide_flops
    )
    other, raised = lax.optimization_barrier((other, raised))
    mine = call(two_kernel, shape(half + PAD), (mine, other, coarse[1]), flops=10**9)
    other = swapped(mine, 1)
    groups = lax.axis_size("grp")
    packet = quarter // groups + PAD
    chosen = call(
        functools.partial(pick_kernel, groups),
        shape(groups * packet),
        (place, top_quarter, mine, other),
        specs=[SM] + [VM] * 3,
        scratch=[wide],
        flops=10**9,
    )
    level_three = pl.pallas_call(
        functools.partial(top_kernel, groups),
        out_shape=shape(slot_rows),
        in_specs=[VM] * 2,
        out_specs=VM,
        scratch_shapes=[
            pltpu.VMEM((groups - 1, packet, features), bf16),
            pltpu.SemaphoreType.DMA((5, groups)),
            pltpu.SemaphoreType.DMA((5, groups)),
        ],
        compiler_params=pltpu.CompilerParams(collective_id=0, has_side_effects=True),
    )(chosen, coarse[2])
    return call(
        last_kernel,
        shape(slot_rows),
        (place, to_two, to_three, raised, mine, other, level_three),
        specs=[SM] + [VM] * 6,
        flops=2 * wide_flops,
    )


def solution(mesh):
    in_specs = (
        P(("sub", "grp"), None),
        P(("sub", "grp")),
        P("sub", "grp", None, None),
        P("sub", "grp", None, None),
        P("sub", "grp", None),
        P(None, "grp", None),
        P(None, "grp", None),
        P(),
        P(),
        P(),
        P(),
        P(),
        P(),
        P(),
        P(),
    )
    out_specs = P(("sub", "grp"), None)
    return jax.shard_map(body, mesh=mesh, in_specs=in_specs, out_specs=out_specs, check_vma=False)
```
